256 devices in a mesh: feat: 32 (over y, z), dp: 8 (over x, core).
Axes of the slice: x: 4, y: 4, z: 8, core: 2. Of those that a mesh axis runs over, the one named last changes fastest.
Arguments:
- query_grads: bfloat16 [512, 131072], P(('dp', 'feat')), may hold values from -52 to 52
- build_grads: bfloat16 [1024, 131072], P('dp', 'feat'), may hold values from -52 to 52
- scored_grads: bfloat16 [4096, 131072], P('dp', 'feat'), may hold values from -52 to 52
Outputs:
- scores: float32 [4096, 512], P(('dp', 'feat'))
The draws below stay inside these ranges and needn't reach their ends.
All inputs are finite; a program needn't handle non-finite values.
Results may differ from the reference program's by a relative error of at most 0.0049.
Values may be sent and summed in bfloat16 or wider, within the bound.
No kernel may reach another device: no remote copies, remote signals or barrier semaphores. Data moves between devices by JAX's collectives and lax.ppermute only.
A program may use at most 128 MiB of HBM per device.

```python
import math
import jax
import jax.numpy as jnp
from jax import lax

MATS = 32
FEAT = 131072
NQ = 512
NB = 1024
NS = 4096


def feature_scale(base_key):
    spread = jax.random.uniform(jax.random.fold_in(base_key, 11), (FEAT,), jnp.float32)
    position = jnp.arange(FEAT, dtype=jnp.float32) / FEAT
    return jnp.exp(jnp.log(3.0) * position + jnp.log(3.3) * spread)


def shared_part(base_key, own_key, row_count):
    group_count = MATS * 2
    group_span = FEAT // group_count
    ranking = jax.random.permutation(jax.random.fold_in(base_key, 17), group_count)
    harmonic = math.log(group_count) + 0.5772 + 0.5 / group_count
    strength = jnp.sqrt(group_count / harmonic / (ranking.astype(jnp.float32) + 1.0))
    direction = jnp.clip(jax.random.normal(jax.random.fold_in(base_key, 19), (group_count, group_span), jnp.float32), -4.0, 4.0)
    loadings = jnp.clip(jax.random.normal(jax.random.fold_in(own_key, 3), (row_count, group_count), jnp.float32), -4.0, 4.0)
    blocks = (loadings * strength[None, :])[:, :, None] * direction[None, :, :]
    return blocks.reshape(row_count, FEAT)


def example_rows(base_key, salt_value, row_count):
    own_key = jax.random.fold_in(base_key, salt_value)
    spread = jax.random.uniform(jax.random.fold_in(own_key, 1), (row_count,), jnp.float32)
    position = jnp.arange(row_count, dtype=jnp.float32) / row_count
    row_scale = jnp.exp(jnp.log(10.0) * (0.5 * position + 0.5 * spread))
    shared = shared_part(base_key, own_key, row_count)
    rough_part = jnp.clip(jax.random.normal(jax.random.fold_in(own_key, 2), (row_count, FEAT), jnp.float32), -4.0, 4.0)
    rough_part = jnp.clip(rough_part + 0.23 * shared, -5.0, 5.0)
    overall = 0.1
    values = overall * rough_part * row_scale[:, None] * feature_scale(base_key)[None, :]
    return values.astype(jnp.bfloat16)


def draw_query_grads(key, part):
    return example_rows(key, 101, NQ)


def draw_build_grads(key, part):
    return example_rows(key, 202, NB)


def draw_scored_grads(key, part):
    return example_rows(key, 303, NS)


def setup_inputs(seed: int = 0) -> dict:
    keys = jax.random.split(jax.random.key(seed), 4)
    query_grads = draw_query_grads(jax.random.fold_in(keys[3], 71), 0)
    build_grads = draw_build_grads(jax.random.fold_in(keys[3], 71), 0)
    scored_grads = draw_scored_grads(jax.random.fold_in(keys[3], 71), 0)
    return {"query_grads": query_grads, "build_grads": build_grads, "scored_grads": scored_grads}


def reference(query_grads, build_grads, scored_grads):
    build_wide = build_grads.astype(jnp.float32)
    damping = 0.1 * jnp.sum(build_wide * build_wide) / (NB * FEAT) + 1e-06
    gram_matrix = jnp.dot(build_grads.astype(jnp.float32), build_grads.T.astype(jnp.float32), preferred_element_type=jnp.float32)
    gram_matrix = gram_matrix + NB * damping * jnp.eye(NB, dtype=jnp.float32)
    cross_sums = jnp.dot(build_grads.astype(jnp.float32), query_grads.T.astype(jnp.float32), preferred_element_type=jnp.float32)
    factor = jnp.linalg.cholesky(gram_matrix)
    solved = jax.scipy.linalg.cho_solve((factor, True), cross_sums)
    solved_half = solved.astype(jnp.bfloat16)
    query_wide = query_grads.astype(jnp.float32)
    precond = (query_wide - jnp.dot(solved_half.T.astype(jnp.float32), build_grads.astype(jnp.float32), preferred_element_type=jnp.float32)) / damping
    self_score = lax.optimization_barrier(jnp.sum(query_wide * precond, axis=1))
    normed = (precond / jnp.sqrt(self_score)[:, None]).astype(jnp.bfloat16)
    return jnp.dot(scored_grads.astype(jnp.float32), normed.T.astype(jnp.float32), preferred_element_type=jnp.float32)
```

```python
import functools
import jax, jax.numpy as jnp
from jax import lax
from jax.experimental import pallas as pl
from jax.experimental.pallas import tpu as pltpu

BLK = 128
BF = jnp.bfloat16
F32 = jnp.float32

def split3(x):
    h = x.astype(BF)
    r = x - h.astype(F32)
    m = r.astype(BF)
    l = (r - m.astype(F32)).astype(BF)
    return h, m, l

def cat_left(x):
    h, m, l = split3(x)
    return jnp.concatenate([h, h, m, h, l, m], axis=1)

def cat_right(x):
    h, m, l = split3(x)
    return jnp.concatenate([h, m, h, l, h, m], axis=0)

def mm(a, b):
    return jnp.dot(a, b, preferred_element_type=F32)

def inverse(a):
    n = a.shape[0]
    lane = lax.broadcasted_iota(jnp.int32, (1, n), 1)
    for j in range(0, n, 2):
        c0 = jnp.broadcast_to(a[:, j:j+1], (n, n))
        c1 = jnp.broadcast_to(a[:, j+1:j+2], (n, n))
        p, q, s = c0[j:j+1], c0[j+1:j+2], c1[j+1:j+2]
        inv = 1.0 / (p * s - q * q)
        i00, i01, i11 = s * inv, -q * inv, p * inv
        r0 = jnp.where(lane == j, 1.0, jnp.where(lane == j + 1, 0.0, a[j:j+1]))
        r1 = jnp.where(lane == j, 0.0, jnp.where(lane == j + 1, 1.0, a[j+1:j+2]))
        t0 = i00 * r0 + i01 * r1
        t1 = i01 * r0 + i11 * r1
        keep = (lane == j) | (lane == j + 1)
        base = jnp.where(keep, 0.0, a)
        new = base - c0 * t0 - c1 * t1
        parts = []
        if j: parts.append(new[:j])
        parts += [t0, t1]
        if j + 2 < n: parts.append(new[j+2:])
        a = jnp.concatenate(parts, axis=0)
    return a

def solve_kernel(n, nq, m_ref, x_ref, dots_ref, damp_ref, a, t, dinv, w, lc):
    g = n // BLK
    qs = nq // g
    tot = jnp.zeros((BLK, BLK), F32)
    eye = (lax.broadcasted_iota(jnp.int32, (BLK, BLK), 0) == lax.broadcasted_iota(jnp.int32, (BLK, BLK), 1)).astype(F32)
    for k in range(g):
        for c in range(n // 256):
            a[k*BLK:(k+1)*BLK, c*256:(c+1)*256] = m_ref[k, c, :BLK, :]
            t[k*qs:(k+1)*qs, c*256:(c+1)*256] = m_ref[k, c, BLK:, :]
        tot = tot + a[k*BLK:(k+1)*BLK, k*BLK:(k+1)*BLK] * eye
    trace = jnp.sum(jnp.sum(tot, axis=1, keepdims=True), axis=0, keepdims=True)
    damping = 0.1 * trace / (n * 131072) + 1e-06
    damp_ref[...] = jnp.broadcast_to(damping, (8, 128))
    for k in range(g):
        s = slice(k*BLK, (k+1)*BLK)
        a[s, s] = a[s, s] + eye * (n * damping)
    tiles = n // 256

    def update(ref, rt, ct):
        rs = pl.ds(pl.multiple_of(rt * 256, 256), 256)
        cs = pl.ds(pl.multiple_of(ct * 256, 256), 256)
        ref[rs, cs] = ref[rs, cs] - mm(lc[rs, :], w[:, cs])

    def set_left(ref, rt, ks):
        rs = pl.ds(pl.multiple_of(rt * 256, 256), 256)
        lc[rs, :] = cat_left(ref[rs, ks])

    col = lax.broadcasted_iota(jnp.int32, (1, n), 1)

    def forward(k, _):
        ks = pl.ds(pl.multiple_of(k * BLK, BLK), BLK)
        d = inverse(a[ks, ks])
        dinv[ks, :] = d
        lo = (k + 1) // 2
        dl = cat_left(d)
        def make_w(ct, _):
            cs = pl.ds(pl.multiple_of(ct * 256, 256), 256)
            cc = lax.broadcasted_iota(jnp.int32, (1, 256), 1) + ct * 256
            v = mm(dl, cat_right(a[ks, cs]))
            w[:, cs] = cat_right(jnp.where(cc >= (k + 1) * BLK, v, 0.0))
            return 0
        lax.fori_loop(lo, tiles, make_w, 0)
        def rows_a(rt, _):
            set_left(a, rt, ks)
            def cols(ct, _):
                update(a, rt, ct)
                return 0
            return lax.fori_loop(lo, tiles, cols, 0)
        lax.fori_loop(lo, tiles, rows_a, 0)
        def rows_t(rt, _):
            set_left(t, rt, ks)
            def cols(ct, _):
                update(t, rt, ct)
                return 0
            return lax.fori_loop(lo, tiles, cols, 0)
        lax.fori_loop(0, nq // 256, rows_t, 0)
        return 0
    lax.fori_loop(0, g, forward, 0)

    def backward(i, _):
        k = g - 1 - i
        ks = pl.ds(pl.multiple_of(k * BLK, BLK), BLK)
        dr = cat_right(dinv[ks, :])
        hi = (k + 1) // 2
        def make_w(ct, _):
            cs = pl.ds(pl.multiple_of(ct * 256, 256), 256)
            cc = lax.broadcasted_iota(jnp.int32, (1, 256), 1) + ct * 256
            w[:, cs] = cat_right(jnp.where(cc < k * BLK, a[ks, cs], 0.0))
            return 0
        lax.fori_loop(0, hi, make_w, 0)
        def rows_t(rt, _):
            rs = pl.ds(pl.multiple_of(rt * 256, 256), 256)
            x = mm(cat_left(t[rs, ks]), dr)
            t[rs, ks] = x
            lc[rs, :] = cat_left(x)
            def cols(ct, _):
                update(t, rt, ct)
                return 0
            return lax.fori_loop(0, hi, cols, 0)
        lax.fori_loop(0, nq // 256, rows_t, 0)
        return 0
    lax.fori_loop(0, g, backward, 0)
    for k in range(g):
        xs = t[k*qs:(k+1)*qs, :].astype(BF)
        x_ref[k*qs:(k+1)*qs, :] = xs
        acc = jnp.zeros((qs, 256), F32)
        for c in range(n // 256):
            acc = acc + xs[:, c*256:(c+1)*256].astype(F32) * m_ref[k, c, BLK:, :]
        dots_ref[k*qs:(k+1)*qs, :] = jnp.broadcast_to(jnp.sum(acc, axis=1, keepdims=True), (qs, 128))

def solve(m):
    g, chunks, rows, _ = m.shape
    n = chunks * 256
    nq = g * (rows - BLK)
    vm = pl.BlockSpec(memory_space=pltpu.VMEM)
    return pl.pallas_call(
        functools.partial(solve_kernel, n, nq),
        out_shape=(jax.ShapeDtypeStruct((nq, n), BF), jax.ShapeDtypeStruct((nq, 128), F32), jax.ShapeDtypeStruct((8, 128), F32)),
        in_specs=[vm], out_specs=(vm, vm, vm),
        scratch_shapes=[pltpu.VMEM((n, n), F32), pltpu.VMEM((nq, n), F32), pltpu.VMEM((n, BLK), F32),
                        pltpu.VMEM((6*BLK, n), BF), pltpu.VMEM((max(n, nq), 6*BLK), BF)],
        compiler_params=pltpu.CompilerParams(vmem_limit_bytes=56 * 1024 * 1024),
        cost_estimate=pl.CostEstimate(flops=20_000_000_000, bytes_accessed=8_000_000, transcendentals=0),
        name="solve",
    )(m)


from jax.sharding import Mesh
from jax.sharding import PartitionSpec as P

FEAT = 131072
FEAT_AXES = ("feat_0", "feat_1")
DP = ("dp_0", "dp_1")
DP_FEAT = ("dp_0", "dp_1", "feat_0", "feat_1")


def contract_last(left, right):
    return lax.dot_general(left, right, (((1,), (1,)), ((), ())), preferred_element_type=F32)


def on_device(query_grads, build_grads, scored_grads):
    q_local = lax.all_to_all(query_grads, FEAT_AXES, split_axis=1, concat_axis=0, tiled=True)
    build_all = lax.all_gather(build_grads, DP, axis=0, tiled=True)
    rows = jnp.concatenate([build_grads, q_local], axis=0)
    query_wide = q_local.astype(F32)
    own_squares = jnp.sum(query_wide * query_wide, axis=1)
    slot = lax.axis_index(DP)
    squares = jnp.zeros((lax.axis_size(DP), own_squares.shape[0]), F32).at[slot].set(own_squares)
    squares = lax.psum(squares.reshape(-1), FEAT_AXES + DP)
    squares, rows = lax.optimization_barrier((squares, rows))
    build_rows = build_all.shape[0]
    sums = jnp.concatenate([contract_last(rows, build_all[c:c + 256]) for c in range(0, build_rows, 256)], axis=0)
    sums = lax.psum_scatter(sums, FEAT_AXES, scatter_dimension=0, tiled=True)
    score_build = contract_last(scored_grads, build_all)
    high = lax.reduce_precision(score_build, 8, 7)
    low = (score_build - high).astype(BF)
    pair = jnp.concatenate([high.astype(BF), low], axis=1)
    sums, pair = lax.optimization_barrier((sums, pair))
    sums = lax.all_gather(sums, DP_FEAT, axis=0, tiled=True)
    q_local, sums = lax.optimization_barrier((q_local, sums))
    query_all = lax.all_gather(q_local, DP, axis=0, tiled=True)
    half, dots, damp = solve(sums.reshape(build_rows // BLK, build_rows // 256, -1, 256))
    damping = damp[0, 0]
    self_score = (squares - dots[:, 0]) / damping
    scale = 1.0 / (damping * jnp.sqrt(self_score))
    score_query = contract_last(scored_grads, query_all)
    removed = contract_last(pair, jnp.concatenate([half, half], axis=1))
    partial_value = (score_query - removed) * scale[None, :]
    return lax.psum_scatter(partial_value, FEAT_AXES, scatter_dimension=0, tiled=True)


def solution(mesh):
    torus = Mesh(mesh.devices.reshape(4, 8, 4, 2), ("feat_0", "feat_1", "dp_0", "dp_1"))
    in_specs = (P(DP_FEAT, None), P(DP, FEAT_AXES), P(DP, FEAT_AXES))
    out_specs = P(DP_FEAT, None)
    return jax.shard_map(
        on_device, mesh=torus, in_specs=in_specs, out_specs=out_specs, check_vma=False
    )
```

```python
import functools
import jax, jax.numpy as jnp
from jax import lax
from jax.experimental import pallas as pl
from jax.experimental.pallas import tpu as pltpu

BLK = 128
FEAT = 131072
BF = jnp.bfloat16
F32 = jnp.float32

def split3(x):
    h = x.astype(BF)
    r = x - h.astype(F32)
    m = r.astype(BF)
    l = (r - m.astype(F32)).astype(BF)
    return h, m, l

def cat_left(x):
    h, m, l = split3(x)
    return jnp.concatenate([h, h, m, h, l, m], axis=1)

def cat_right(x):
    h, m, l = split3(x)
    return jnp.concatenate([h, m, h, l, h, m], axis=0)

def mm(a, b):
    return jnp.dot(a, b, preferred_element_type=F32)

def put_rows(x, j, row0, row1):
    g = j // 8 * 8
    sub = lax.broadcasted_iota(jnp.int32, (8, x.shape[1]), 0)
    block = jnp.where(sub == j - g, row0, jnp.where(sub == j - g + 1, row1, x[g:g+8]))
    parts = ([x[:g]] if g else []) + [block] + ([x[g+8:]] if g + 8 < x.shape[0] else [])
    return jnp.concatenate(parts, axis=0)

def sweep(p, off):
    rows = p.shape[0]
    lane = lax.broadcasted_iota(jnp.int32, (1, p.shape[1]), 1)
    def spread(x, i):
        return jnp.broadcast_to(x[:, i:i+1], x.shape)
    c0, c1 = spread(p, off), spread(p, off + 1)
    for j in range(0, rows, 2):
        e, f, h = c0[j:j+1], c0[j+1:j+2], c1[j+1:j+2]
        inv = 1.0 / (e * h - f * f)
        i00, i01, i11 = h * inv, -f * inv, e * inv
        more = j + 2 < rows
        if more:
            d0, d1 = spread(p, off + j + 2), spread(p, off + j + 3)
            x0, x1 = c0[j+2:j+3], c1[j+2:j+3]
            y0, y1 = c0[j+3:j+4], c1[j+3:j+4]
            u0, u1 = i00 * x0 + i01 * x1, i01 * x0 + i11 * x1
            v0, v1 = i00 * y0 + i01 * y1, i01 * y0 + i11 * y1
            n0 = put_rows(d0 - c0 * u0 - c1 * u1, j, u0, u1)
            n1 = put_rows(d1 - c0 * v0 - c1 * v1, j, v0, v1)
        first, second = lane == off + j, lane == off + j + 1
        r0 = jnp.where(first, 1.0, jnp.where(second, 0.0, p[j:j+1]))
        r1 = jnp.where(first, 0.0, jnp.where(second, 1.0, p[j+1:j+2]))
        t0 = i00 * r0 + i01 * r1
        t1 = i01 * r0 + i11 * r1
        p = put_rows(jnp.where(first | second, 0.0, p) - c0 * t0 - c1 * t1, j, t0, t1)
        if more:
            c0, c1 = n0, n1
    return p

def inverse(a):
    n = a.shape[0]
    h = n // 2
    left = lax.broadcasted_iota(jnp.int32, (1, n), 1) < h
    top = sweep(a[:h], 0)
    low = jnp.where(left, 0.0, a[h:]) - mm(cat_left(a[h:, :h]), cat_right(top))
    low = sweep(low, h)
    high = jnp.where(left, top, 0.0) - mm(cat_left(top[:, h:]), cat_right(low))
    return jnp.concatenate([high, low], axis=0)

def across(a, b):
    return lax.dot_general(a, b, (((1,), (1,)), ((), ())), preferred_element_type=F32)

def solve_kernel(n, nq, m_ref, sb_ref, sq_ref, out_ref, a, t, dinv, w, lc, w2):
    g = n // BLK
    qs = nq // g
    rows = BLK + qs
    chunks = n // 256
    tot = jnp.zeros((BLK, BLK), F32)
    eye = (lax.broadcasted_iota(jnp.int32, (BLK, BLK), 0) == lax.broadcasted_iota(jnp.int32, (BLK, BLK), 1)).astype(F32)
    for k in range(g):
        for c in range(chunks):
            a[k*BLK:(k+1)*BLK, c*256:(c+1)*256] = m_ref[k, c*rows:c*rows+BLK, :]
            t[k*qs:(k+1)*qs, c*256:(c+1)*256] = m_ref[k, c*rows+BLK:(c+1)*rows, :]
        tot = tot + a[k*BLK:(k+1)*BLK, k*BLK:(k+1)*BLK] * eye
    trace = jnp.sum(jnp.sum(tot, axis=1, keepdims=True), axis=0, keepdims=True)
    damping = 0.1 * trace / (n * FEAT) + 1e-06
    for k in range(g):
        s = slice(k*BLK, (k+1)*BLK)
        a[s, s] = a[s, s] + eye * (n * damping)
    tiles = n // 256

    def update(ref, rt, ct):
        rs = pl.ds(pl.multiple_of(rt * 256, 256), 256)
        cs = pl.ds(pl.multiple_of(ct * 256, 256), 256)
        ref[rs, cs] = ref[rs, cs] - mm(lc[rs, :], w[:, cs])

    def set_left(ref, rt, ks):
        rs = pl.ds(pl.multiple_of(rt * 256, 256), 256)
        lc[rs, :] = cat_left(ref[rs, ks])

    col = lax.broadcasted_iota(jnp.int32, (1, n), 1)

    def forward(k, _):
        ks = pl.ds(pl.multiple_of(k * BLK, BLK), BLK)
        d = inverse(a[ks, ks])
        dinv[ks, :] = d
        lo = (k + 1) // 2
        dl = cat_left(d)
        def make_w(ct, _):
            cs = pl.ds(pl.multiple_of(ct * 256, 256), 256)
            cc = lax.broadcasted_iota(jnp.int32, (1, 256), 1) + ct * 256
            v = mm(dl, cat_right(a[ks, cs]))
            w[:, cs] = cat_right(jnp.where(cc >= (k + 1) * BLK, v, 0.0))
            return 0
        lax.fori_loop(lo, tiles, make_w, 0)
        def rows_a(rt, _):
            set_left(a, rt, ks)
            def cols(ct, _):
                update(a, rt, ct)
                return 0
            return lax.fori_loop(lo, tiles, cols, 0)
        lax.fori_loop(lo, tiles, rows_a, 0)
        def rows_t(rt, _):
            set_left(t, rt, ks)
            def cols(ct, _):
                update(t, rt, ct)
                return 0
            return lax.fori_loop(lo, tiles, cols, 0)
        lax.fori_loop(0, nq // 256, rows_t, 0)
        return 0
    lax.fori_loop(0, g, forward, 0)

    def backward(i, _):
        k = g - 1 - i
        ks = pl.ds(pl.multiple_of(k * BLK, BLK), BLK)
        dr = cat_right(dinv[ks, :])
        hi = (k + 1) // 2
        def make_w(ct, _):
            cs = pl.ds(pl.multiple_of(ct * 256, 256), 256)
            cc = lax.broadcasted_iota(jnp.int32, (1, 256), 1) + ct * 256
            w[:, cs] = cat_right(jnp.where(cc < k * BLK, a[ks, cs], 0.0))
            return 0
        lax.fori_loop(0, hi, make_w, 0)
        def rows_t(rt, _):
            rs = pl.ds(pl.multiple_of(rt * 256, 256), 256)
            x = mm(cat_left(t[rs, ks]), dr)
            t[rs, ks] = x
            lc[rs, :] = cat_left(x)
            def cols(ct, _):
                update(t, rt, ct)
                return 0
            return lax.fori_loop(0, hi, cols, 0)
        lax.fori_loop(0, nq // 256, rows_t, 0)
        return 0
    lax.fori_loop(0, g, backward, 0)
    ones = jnp.ones((8, 768), BF)
    squares = jnp.zeros((8, 256), F32)
    for k in range(g):
        squares = squares + m_ref[k, chunks*rows:chunks*rows+8, :]
    scales = []
    for h in range(nq // 256):
        accs = []
        for k in range(h * 256 // qs, (h + 1) * 256 // qs):
            acc = jnp.zeros((qs, 256), F32)
            for c in range(chunks):
                x = t[k*qs:(k+1)*qs, c*256:(c+1)*256].astype(BF)
                w2[k*qs:(k+1)*qs, c*256:(c+1)*256] = x
                acc = acc + x.astype(F32) * m_ref[k, c*rows+BLK:(c+1)*rows, :]
            accs.append(acc)
        parts = split3(jnp.concatenate(accs, axis=0))
        dots = across(ones, jnp.concatenate(parts, axis=1))[:1]
        self_score = (squares[h:h+1] - dots) / damping
        scales.append(1.0 / (damping * jnp.sqrt(self_score)))
    def finish(rt, _):
        rs = pl.ds(pl.multiple_of(rt * 128, 128), 128)
        wide = sb_ref[rs, :]
        high = wide.astype(BF)
        low = (wide - high.astype(F32)).astype(BF)
        for h in range(nq // 256):
            hs = slice(h * 256, (h + 1) * 256)
            removed = across(high, w2[hs, :]) + across(low, w2[hs, :])
            out_ref[rs, hs] = ((sq_ref[rs, hs] - removed) * scales[h]).astype(BF)
        return 0
    lax.fori_loop(0, sb_ref.shape[0] // 128, finish, 0)

def solve(m, sb, sq):
    g = m.shape[0]
    ns, n = sb.shape
    nq = sq.shape[1]
    vm = pl.BlockSpec(memory_space=pltpu.VMEM)
    return pl.pallas_call(
        functools.partial(solve_kernel, n, nq),
        out_shape=jax.ShapeDtypeStruct((ns, nq), BF),
        in_specs=[vm] * 3, out_specs=vm,
        scratch_shapes=[pltpu.VMEM((n, n), F32), pltpu.VMEM((nq, n), F32), pltpu.VMEM((n, BLK), F32),
                        pltpu.VMEM((6*BLK, n), BF), pltpu.VMEM((max(n, nq), 6*BLK), BF), pltpu.VMEM((nq, n), BF)],
        compiler_params=pltpu.CompilerParams(vmem_limit_bytes=48 * 1024 * 1024),
        cost_estimate=pl.CostEstimate(flops=20_000_000_000, bytes_accessed=12_000_000, transcendentals=0),
        name="solve",
    )(m, sb, sq)


from jax.sharding import Mesh
from jax.sharding import PartitionSpec as P

FEAT_AXES = ("feat_0", "feat_1")
DP = ("dp_0", "dp_1")
DP_FEAT = ("dp_0", "dp_1", "feat_0", "feat_1")


def exchange(x):
    return lax.all_to_all(x, FEAT_AXES, 0, 0, tiled=True)


def on_device(query_grads, build_grads, scored_grads):
    q_local = lax.all_to_all(query_grads, FEAT_AXES, split_axis=1, concat_axis=0, tiled=True)
    build_all = lax.all_gather(build_grads, DP, axis=0, tiled=True)
    build_rows = build_all.shape[0]
    query_wide = q_local.astype(F32)
    squares = jnp.sum(query_wide * query_wide, axis=1)
    for axis in FEAT_AXES:
        squares = lax.psum(squares, axis)
    per_row = 256 // squares.shape[0]
    slot = lax.axis_index(DP)
    squares = lax.dynamic_update_slice(
        jnp.zeros((8, 256), F32), squares[None], (slot // per_row, slot % per_row * squares.shape[0])
    )
    rows = jnp.concatenate([build_grads, q_local], axis=0)
    squares, rows = lax.optimization_barrier((squares, rows))
    sums = jnp.concatenate([across(rows, build_all[c:c + 256]) for c in range(0, build_rows, 256)], axis=0)
    size = lax.axis_size(FEAT_AXES)
    sums = jnp.sum(exchange(sums.reshape(size, -1, 256)), axis=0)
    sums = exchange(jnp.broadcast_to(sums[None], (size, *sums.shape)))
    sums = jnp.concatenate([sums.reshape(-1, 256), squares], axis=0)
    sums = lax.all_gather(sums, DP, axis=0, tiled=True)
    query_all = lax.all_gather(q_local, DP, axis=0, tiled=True)
    score_query = across(scored_grads, query_all)
    score_build = across(scored_grads, build_all)
    sums, score_query, score_build = lax.optimization_barrier((sums, score_query, score_build))
    partial_value = solve(sums.reshape(build_rows // BLK, -1, 256), score_build, score_query)
    partial_value = exchange(partial_value.reshape(size, -1, partial_value.shape[1]))
    return jnp.sum(partial_value.astype(F32), axis=0)


def solution(mesh):
    torus = Mesh(mesh.devices.reshape(4, 8, 4, 2), ("feat_0", "feat_1", "dp_0", "dp_1"))
    in_specs = (P(DP_FEAT, None), P(DP, FEAT_AXES), P(DP, FEAT_AXES))
    out_specs = P(DP_FEAT, None)
    return jax.shard_map(
        on_device, mesh=torus, in_specs=in_specs, out_specs=out_specs, check_vma=False
    )
```

```python
import functools
import jax, jax.numpy as jnp
from jax import lax
from jax.experimental import pallas as pl
from jax.experimental.pallas import tpu as pltpu

BLK = 128
FEAT = 131072
BF = jnp.bfloat16
F32 = jnp.float32

def split3(x):
    h = x.astype(BF)
    r = x - h.astype(F32)
    m = r.astype(BF)
    l = (r - m.astype(F32)).astype(BF)
    return h, m, l

def split2(x):
    h = x.astype(BF)
    return h, (x - h.astype(F32)).astype(BF)

def left6(x):
    h, m, l = split3(x)
    return jnp.concatenate([h, h, m, m, h, l], axis=1)

def right6(x):
    h, m, l = split3(x)
    return jnp.concatenate([h, m, h, m, l, h], axis=0)

def left4(x):
    h, m = split2(x)
    return jnp.concatenate([h, h, m, m], axis=1)

def mixed4(x):
    h, m = split2(x)
    return jnp.concatenate([h, m, h, m], axis=1)

def mm(a, b):
    return jnp.dot(a, b, preferred_element_type=F32)

def across(a, b):
    return lax.dot_general(a, b, (((1,), (1,)), ((), ())), preferred_element_type=F32)

def put_rows(x, j, row0, row1):
    g = j // 8 * 8
    sub = lax.broadcasted_iota(jnp.int32, (8, x.shape[1]), 0)
    block = jnp.where(sub == j - g, row0, jnp.where(sub == j - g + 1, row1, x[g:g+8]))
    parts = ([x[:g]] if g else []) + [block] + ([x[g+8:]] if g + 8 < x.shape[0] else [])
    return jnp.concatenate(parts, axis=0)

def sweep(p, off, tick):
    rows = p.shape[0]
    lane = lax.broadcasted_iota(jnp.int32, (1, p.shape[1]), 1)
    def spread(x, i):
        return jnp.broadcast_to(x[:, i:i+1], x.shape)
    c0, c1 = spread(p, off), spread(p, off + 1)
    for j in range(0, rows, 2):
        e, f, h = c0[j:j+1], c0[j+1:j+2], c1[j+1:j+2]
        inv = 1.0 / (e * h - f * f)
        i00, i01, i11 = h * inv, -f * inv, e * inv
        more = j + 2 < rows
        if more:
            d0, d1 = spread(p, off + j + 2), spread(p, off + j + 3)
            x0, x1 = c0[j+2:j+3], c1[j+2:j+3]
            y0, y1 = c0[j+3:j+4], c1[j+3:j+4]
            u0, u1 = i00 * x0 + i01 * x1, i01 * x0 + i11 * x1
            v0, v1 = i00 * y0 + i01 * y1, i01 * y0 + i11 * y1
            n0 = put_rows(d0 - c0 * u0 - c1 * u1, j, u0, u1)
            n1 = put_rows(d1 - c0 * v0 - c1 * v1, j, v0, v1)
        first, second = lane == off + j, lane == off + j + 1
        r0 = jnp.where(first, 1.0, jnp.where(second, 0.0, p[j:j+1]))
        r1 = jnp.where(first, 0.0, jnp.where(second, 1.0, p[j+1:j+2]))
        t0 = i00 * r0 + i01 * r1
        t1 = i01 * r0 + i11 * r1
        p = put_rows(jnp.where(first | second, 0.0, p) - c0 * t0 - c1 * t1, j, t0, t1)
        if more:
            c0, c1 = n0, n1
        tick()
    return p

def inverse(a, tick):
    n = a.shape[0]
    h = n // 2
    left = lax.broadcasted_iota(jnp.int32, (1, n), 1) < h
    top = sweep(a[:h], 0, tick)
    low = jnp.where(left, 0.0, a[h:]) - mm(left6(a[h:, :h]), right6(top))
    low = sweep(low, h, tick)
    high = jnp.where(left, top, 0.0) - mm(left6(top[:, h:]), right6(low))
    return jnp.concatenate([high, low], axis=0)

TILE = 256

class Spread:
    def __init__(self, tasks, steps):
        self.tasks, self.steps, self.step, self.done = tasks, steps, 0, 0
    def __call__(self):
        self.step += 1
        upto = len(self.tasks) * self.step // self.steps
        while self.done < upto:
            self.tasks[self.done]()
            self.done += 1

def solve_kernel(n, nq, m_ref, sb_ref, sq_ref, out_ref, a, t, z, s, dinv, w, la, lt, lz, dq):
    g = n // BLK
    ns = sb_ref.shape[0]
    qs = nq // g
    rows = BLK + qs
    chunks = n // 256
    tiles = n // TILE
    tot = jnp.zeros((BLK, BLK), F32)
    eye = (lax.broadcasted_iota(jnp.int32, (BLK, BLK), 0) == lax.broadcasted_iota(jnp.int32, (BLK, BLK), 1)).astype(F32)
    for k in range(g):
        for c in range(chunks):
            a[k*BLK:(k+1)*BLK, c*256:(c+1)*256] = m_ref[k, c*rows:c*rows+BLK, :]
            t[k*qs:(k+1)*qs, c*256:(c+1)*256] = m_ref[k, c*rows+BLK:(c+1)*rows, :]
        tot = tot + a[k*BLK:(k+1)*BLK, k*BLK:(k+1)*BLK] * eye
    trace = jnp.sum(jnp.sum(tot, axis=1, keepdims=True), axis=0, keepdims=True)
    damping = 0.1 * trace / (n * FEAT) + 1e-06
    for k in range(g):
        d = slice(k*BLK, (k+1)*BLK)
        a[d, d] = a[d, d] + eye * (n * damping)
    z[...] = sb_ref[...]
    s[...] = sq_ref[...]
    dq[...] = jnp.zeros(dq.shape, F32)
    dinv[...] = inverse(a[:BLK, :BLK], lambda: None)

    def strip(i):
        return slice(i * TILE, (i + 1) * TILE)

    def score_tasks(ks, d):
        d4 = right6(d)[:4*BLK]
        def dots(rt):
            r = strip(rt)
            lt[r, :] = left4(t[r, ks])
            dq[r, :] = dq[r, :] + mm(lt[r, :], d4) * t[r, ks]
        def scores(rt):
            r = strip(rt)
            lz[r, :] = left4(z[r, ks])
            v = mixed4(mm(lz[r, :], d4))
            for ct in range(nq // TILE):
                c = strip(ct)
                s[r, c] = s[r, c] - across(v, lt[c, :])
        return [functools.partial(dots, i) for i in range(nq // TILE)] + [functools.partial(scores, i) for i in range(ns // TILE)]

    def forward(lo, k, _):
        ks = pl.ds(pl.multiple_of(k * BLK, BLK), BLK)
        ns_ = pl.ds(pl.multiple_of((k + 1) * BLK, BLK), BLK)
        d = dinv[...]
        dl = left6(d)
        near = mm(dl, right6(a[ks, ns_]))
        block = a[ns_, ns_] - mm(left6(a[ns_, ks]), right6(near))

        def make_w(ct):
            c = strip(ct)
            cc = lax.broadcasted_iota(jnp.int32, (1, TILE), 1) + ct * TILE
            w[:, c] = right6(jnp.where(cc >= (k + 1) * BLK, mm(dl, right6(a[ks, c])), 0.0))
        def make_la(rt):
            la[strip(rt), :] = left6(a[strip(rt), ks])
        def update(ref, left, terms, rt, ct):
            r, c = strip(rt), strip(ct)
            ref[r, c] = ref[r, c] - mm(left[r, :], w[:terms*BLK, c])
        tasks = [functools.partial(make_w, i) for i in range(lo, tiles)]
        tasks += [functools.partial(make_la, i) for i in range(lo, tiles)]
        tasks += score_tasks(ks, d)
        for ct in range(lo, tiles):
            tasks += [functools.partial(update, a, la, 6, rt, ct) for rt in range(lo, tiles)]
            tasks += [functools.partial(update, t, lt, 4, rt, ct) for rt in range(nq // TILE)]
            tasks += [functools.partial(update, z, lz, 4, rt, ct) for rt in range(ns // TILE)]
        tick = Spread(tasks, BLK // 2)
        dinv[...] = inverse(block, tick)
        return 0

    for first, last, lo in SECTIONS:
        lax.fori_loop(first, last, functools.partial(forward, lo), 0)
    for task in score_tasks(slice(n - BLK, n), dinv[...]):
        task()

    squares = jnp.zeros((8, 256), F32)
    for k in range(g):
        squares = squares + m_ref[k, chunks*rows:chunks*rows+8, :]
    ones = jnp.ones((8, 3 * BLK), BF)
    for h in range(nq // 256):
        c = strip(h)
        dots = across(ones, jnp.concatenate(split3(dq[c, :]), axis=1))[:1]
        self_score = (squares[h:h+1] - dots) / damping
        out_ref[:, c] = (s[:, c] * (1.0 / (damping * jnp.sqrt(self_score)))).astype(BF)

SECTIONS = ((0, 4, 0), (4, 7, 2))

def solve(m, sb, sq):
    g = m.shape[0]
    ns, n = sb.shape
    nq = sq.shape[1]
    vm = pl.BlockSpec(memory_space=pltpu.VMEM)
    return pl.pallas_call(
        functools.partial(solve_kernel, n, nq),
        out_shape=jax.ShapeDtypeStruct((ns, nq), BF),
        in_specs=[vm] * 3, out_specs=vm,
        scratch_shapes=[pltpu.VMEM((n, n), F32), pltpu.VMEM((nq, n), F32), pltpu.VMEM((ns, n), F32), pltpu.VMEM((ns, nq), F32),
                        pltpu.VMEM((BLK, BLK), F32), pltpu.VMEM((6*BLK, n), BF), pltpu.VMEM((n, 6*BLK), BF),
                        pltpu.VMEM((nq, 4*BLK), BF), pltpu.VMEM((ns, 4*BLK), BF), pltpu.VMEM((nq, BLK), F32)],
        compiler_params=pltpu.CompilerParams(vmem_limit_bytes=48 * 1024 * 1024),
        cost_estimate=pl.CostEstimate(flops=20_000_000_000, bytes_accessed=12_000_000, transcendentals=0),
        name="solve",
    )(m, sb, sq)


from jax.sharding import Mesh
from jax.sharding import PartitionSpec as P

FEAT_AXES = ("feat_0", "feat_1")
DP = ("dp_0", "dp_1")
DP_FEAT = ("dp_0", "dp_1", "feat_0", "feat_1")


def exchange(x):
    return lax.all_to_all(x, FEAT_AXES, 0, 0, tiled=True)


def on_device(query_grads, build_grads, scored_grads):
    q_local = lax.all_to_all(query_grads, FEAT_AXES, split_axis=1, concat_axis=0, tiled=True)
    build_all = lax.all_gather(build_grads, DP, axis=0, tiled=True)
    build_rows = build_all.shape[0]
    query_wide = q_local.astype(F32)
    squares = jnp.sum(query_wide * query_wide, axis=1)
    for axis in FEAT_AXES:
        squares = lax.psum(squares, axis)
    per_row = 256 // squares.shape[0]
    slot = lax.axis_index(DP)
    squares = lax.dynamic_update_slice(
        jnp.zeros((8, 256), F32), squares[None], (slot // per_row, slot % per_row * squares.shape[0])
    )
    rows = jnp.concatenate([build_grads, q_local], axis=0)
    squares, rows = lax.optimization_barrier((squares, rows))
    sums = jnp.concatenate([across(rows, build_all[c:c + 256]) for c in range(0, build_rows, 256)], axis=0)
    size = lax.axis_size(FEAT_AXES)
    sums = jnp.sum(exchange(sums.reshape(size, -1, 256)), axis=0)
    sums = exchange(jnp.broadcast_to(sums[None], (size, *sums.shape)))
    sums = jnp.concatenate([sums.reshape(-1, 256), squares], axis=0)
    sums = lax.all_gather(sums, DP, axis=0, tiled=True)
    query_all = lax.all_gather(q_local, DP, axis=0, tiled=True)
    score_query = across(scored_grads, query_all)
    score_build = across(scored_grads, build_all)
    sums, score_query, score_build = lax.optimization_barrier((sums, score_query, score_build))
    partial_value = solve(sums.reshape(build_rows // BLK, -1, 256), score_build, score_query)
    partial_value = exchange(partial_value.reshape(size, -1, partial_value.shape[1]))
    return jnp.sum(partial_value.astype(F32), axis=0)


def solution(mesh):
    torus = Mesh(mesh.devices.reshape(4, 8, 4, 2), ("feat_0", "feat_1", "dp_0", "dp_1"))
    in_specs = (P(DP_FEAT, None), P(DP, FEAT_AXES), P(DP, FEAT_AXES))
    out_specs = P(DP_FEAT, None)
    return jax.shard_map(
        on_device, mesh=torus, in_specs=in_specs, out_specs=out_specs, check_vma=False
    )
```

```python
import functools
import jax, jax.numpy as jnp
from jax import lax
from jax.experimental import pallas as pl
from jax.experimental.pallas import tpu as pltpu

BLK = 128
FEAT = 131072
BF = jnp.bfloat16
F32 = jnp.float32

def split3(x):
    h = x.astype(BF)
    r = x - h.astype(F32)
    m = r.astype(BF)
    l = (r - m.astype(F32)).astype(BF)
    return h, m, l

def split2(x):
    h = x.astype(BF)
    return h, (x - h.astype(F32)).astype(BF)

def left6(x):
    h, m, l = split3(x)
    return jnp.concatenate([h, h, m, m, h, l], axis=1)

def right6(x):
    h, m, l = split3(x)
    return jnp.concatenate([h, m, h, m, l, h], axis=0)

def left4(x):
    h, m = split2(x)
    return jnp.concatenate([h, h, m, m], axis=1)

def mixed4(x):
    h, m = split2(x)
    return jnp.concatenate([h, m, h, m], axis=1)

def mm(a, b):
    return jnp.dot(a, b, preferred_element_type=F32)

def across(a, b):
    return lax.dot_general(a, b, (((1,), (1,)), ((), ())), preferred_element_type=F32)

def put_rows(x, j, row0, row1):
    g = j // 8 * 8
    sub = lax.broadcasted_iota(jnp.int32, (8, x.shape[1]), 0)
    block = jnp.where(sub == j - g, row0, jnp.where(sub == j - g + 1, row1, x[g:g+8]))
    parts = ([x[:g]] if g else []) + [block] + ([x[g+8:]] if g + 8 < x.shape[0] else [])
    return jnp.concatenate(parts, axis=0)

def sweep(p, off, tick):
    rows = p.shape[0]
    lane = lax.broadcasted_iota(jnp.int32, (1, p.shape[1]), 1)
    def spread(x, i):
        return jnp.broadcast_to(x[:, i:i+1], x.shape)
    c0, c1 = spread(p, off), spread(p, off + 1)
    for j in range(0, rows, 2):
        e, f, h = c0[j:j+1], c0[j+1:j+2], c1[j+1:j+2]
        inv = 1.0 / (e * h - f * f)
        i00, i01, i11 = h * inv, -f * inv, e * inv
        more = j + 2 < rows
        if more:
            d0, d1 = spread(p, off + j + 2), spread(p, off + j + 3)
            x0, x1 = c0[j+2:j+3], c1[j+2:j+3]
            y0, y1 = c0[j+3:j+4], c1[j+3:j+4]
            u0, u1 = i00 * x0 + i01 * x1, i01 * x0 + i11 * x1
            v0, v1 = i00 * y0 + i01 * y1, i01 * y0 + i11 * y1
            n0 = put_rows(d0 - c0 * u0 - c1 * u1, j, u0, u1)
            n1 = put_rows(d1 - c0 * v0 - c1 * v1, j, v0, v1)
        first, second = lane == off + j, lane == off + j + 1
        r0 = jnp.where(first, 1.0, jnp.where(second, 0.0, p[j:j+1]))
        r1 = jnp.where(first, 0.0, jnp.where(second, 1.0, p[j+1:j+2]))
        t0 = i00 * r0 + i01 * r1
        t1 = i01 * r0 + i11 * r1
        p = put_rows(jnp.where(first | second, 0.0, p) - c0 * t0 - c1 * t1, j, t0, t1)
        if more:
            c0, c1 = n0, n1
        tick()
    return p

def inverse(a, tick):
    n = a.shape[0]
    h = n // 2
    left = lax.broadcasted_iota(jnp.int32, (1, n), 1) < h
    top = sweep(a[:h], 0, tick)
    low = jnp.where(left, 0.0, a[h:]) - mm(left6(a[h:, :h]), right6(top))
    low = sweep(low, h, tick)
    high = jnp.where(left, top, 0.0) - mm(left6(top[:, h:]), right6(low))
    return jnp.concatenate([high, low], axis=0)

TILE = 256

class Spread:
    def __init__(self, tasks, steps):
        self.tasks, self.steps, self.step, self.done = tasks, steps, 0, 0
    def __call__(self):
        self.step += 1
        upto = len(self.tasks) * self.step // self.steps
        while self.done < upto:
            self.tasks[self.done]()
            self.done += 1

def solve_kernel(n, nq, place_ref, *refs):
    pieces, (sb_ref, sq_ref, out_ref, a, t, z, s, dinv, w, la, lt, lz, dq) = refs[:10], refs[10:]
    g = n // BLK
    ns = sb_ref.shape[0]
    qs = nq // g
    rows = BLK + qs
    tiles = n // TILE
    chip, core = place_ref[0], place_ref[1]
    chips = n // 256
    for dx in range(chips):
        there = lax.rem(chip + dx, chips)
        sc = pl.ds(pl.multiple_of(there * 2 * qs, 2 * qs), 2 * qs)
        zc = pl.ds(pl.multiple_of(there * 256, 256), 256)
        def score_rows(i, _, dx=dx, sc=sc, zc=zc):
            r = pl.ds(pl.multiple_of(i * 64, 64), 64)
            s[r, sc] = sq_ref[r, dx*2*qs:(dx+1)*2*qs]
            z[r, zc] = sb_ref[r, dx*256:(dx+1)*256]
            return 0
        lax.fori_loop(0, ns // 64, score_rows, 0)
        for flip in range(2):
            k = there * 2 + lax.rem(core + flip, 2)
            ks = pl.ds(pl.multiple_of(k * BLK, BLK), BLK)
            ts = pl.ds(pl.multiple_of(k * qs, qs), qs)
            if dx == 2:
                refs = [(pieces[4 + 2 * flip], 0), (pieces[5 + 2 * flip], chips // 2)]
            else:
                refs = [(pieces[dx * 2 + flip + (2 if dx > 2 else 0)], 0)]
            for ref, base in refs:
                def columns(c, _, ref=ref, base=base, ks=ks, ts=ts):
                    cs = pl.ds(pl.multiple_of((base + c) * 256, 256), 256)
                    a[ks, cs] = ref[pl.ds(pl.multiple_of(c * rows, 8), BLK), :]
                    t[ts, cs] = ref[pl.ds(pl.multiple_of(c * rows + BLK, 8), qs), :]
                    return 0
                lax.fori_loop(0, ref.shape[0] // rows, columns, 0)
    tot = jnp.zeros((BLK, BLK), F32)
    eye = (lax.broadcasted_iota(jnp.int32, (BLK, BLK), 0) == lax.broadcasted_iota(jnp.int32, (BLK, BLK), 1)).astype(F32)
    blocks = [slice(k*BLK, (k+1)*BLK) for k in range(g)]
    squares = []
    for k in range(g):
        after = blocks[(k + 1) % g]
        squares.append(a[k*BLK:k*BLK+1, after][:, :qs])
        a[blocks[k], after] = jnp.transpose(a[after, blocks[k]])
        tot = tot + a[blocks[k], blocks[k]] * eye
    per = 256 // qs
    squares = [jnp.concatenate(squares[h*per:(h+1)*per], axis=1) for h in range(nq // 256)]
    trace = jnp.sum(jnp.sum(tot, axis=1, keepdims=True), axis=0, keepdims=True)
    damping = 0.1 * trace / (n * FEAT) + 1e-06
    for d in blocks:
        a[d, d] = a[d, d] + eye * (n * damping)
    dq[...] = jnp.zeros(dq.shape, F32)
    dinv[...] = inverse(a[:BLK, :BLK], lambda: None)

    def strip(i):
        return slice(i * TILE, (i + 1) * TILE)

    def score_tasks(ks, d):
        d4 = right6(d)[:4*BLK]
        def dots(rt):
            r = strip(rt)
            lt[r, :] = left4(t[r, ks])
            dq[r, :] = dq[r, :] + mm(lt[r, :], d4) * t[r, ks]
        def scores(rt):
            r = strip(rt)
            lz[r, :] = left4(z[r, ks])
            v = mixed4(mm(lz[r, :], d4))
            for ct in range(nq // TILE):
                c = strip(ct)
                s[r, c] = s[r, c] - across(v, lt[c, :])
        return [functools.partial(dots, i) for i in range(nq // TILE)] + [functools.partial(scores, i) for i in range(ns // TILE)]

    def forward(lo, k, _):
        ks = pl.ds(pl.multiple_of(k * BLK, BLK), BLK)
        ns_ = pl.ds(pl.multiple_of((k + 1) * BLK, BLK), BLK)
        d = dinv[...]
        dl = left6(d)
        near = mm(dl, right6(a[ks, ns_]))
        block = a[ns_, ns_] - mm(left6(a[ns_, ks]), right6(near))

        def make_w(ct):
            c = strip(ct)
            cc = lax.broadcasted_iota(jnp.int32, (1, TILE), 1) + ct * TILE
            w[:, c] = right6(jnp.where(cc >= (k + 1) * BLK, mm(dl, right6(a[ks, c])), 0.0))
        def make_la(rt):
            la[strip(rt), :] = left6(a[strip(rt), ks])
        def update(ref, left, terms, rt, ct):
            r, c = strip(rt), strip(ct)
            ref[r, c] = ref[r, c] - mm(left[r, :], w[:terms*BLK, c])
        tasks = [functools.partial(make_w, i) for i in range(lo, tiles)]
        tasks += [functools.partial(make_la, i) for i in range(lo, tiles)]
        tasks += score_tasks(ks, d)
        for ct in range(lo, tiles):
            tasks += [functools.partial(update, a, la, 6, rt, ct) for rt in range(lo, tiles)]
            tasks += [functools.partial(update, t, lt, 4, rt, ct) for rt in range(nq // TILE)]
            tasks += [functools.partial(update, z, lz, 4, rt, ct) for rt in range(ns // TILE)]
        tick = Spread(tasks, BLK // 2)
        dinv[...] = inverse(block, tick)
        return 0

    for first, last, lo in SECTIONS:
        lax.fori_loop(first, last, functools.partial(forward, lo), 0)
    for task in score_tasks(slice(n - BLK, n), dinv[...]):
        task()

    ones = jnp.ones((8, 3 * BLK), BF)
    for h in range(nq // 256):
        c = strip(h)
        dots = across(ones, jnp.concatenate(split3(dq[c, :]), axis=1))[:1]
        self_score = (squares[h] - dots) / damping
        out_ref[:, c] = (s[:, c] * (1.0 / (damping * jnp.sqrt(self_score)))).astype(BF)

SECTIONS = ((0, 4, 0), (4, 7, 2))

def solve(place, pieces, sb, sq):
    ns, n = sb.shape
    nq = sq.shape[1]
    vm = pl.BlockSpec(memory_space=pltpu.VMEM)
    return pl.pallas_call(
        functools.partial(solve_kernel, n, nq),
        out_shape=jax.ShapeDtypeStruct((ns, nq), BF),
        in_specs=[pl.BlockSpec(memory_space=pltpu.SMEM)] + [vm] * 12, out_specs=vm,
        scratch_shapes=[pltpu.VMEM((n, n), F32), pltpu.VMEM((nq, n), F32), pltpu.VMEM((ns, n), F32), pltpu.VMEM((ns, nq), F32),
                        pltpu.VMEM((BLK, BLK), F32), pltpu.VMEM((6*BLK, n), BF), pltpu.VMEM((n, 6*BLK), BF),
                        pltpu.VMEM((nq, 4*BLK), BF), pltpu.VMEM((ns, 4*BLK), BF), pltpu.VMEM((nq, BLK), F32)],
        compiler_params=pltpu.CompilerParams(vmem_limit_bytes=48 * 1024 * 1024),
        cost_estimate=pl.CostEstimate(flops=20_000_000_000, bytes_accessed=12_000_000, transcendentals=0),
        name="solve",
    )(place, *pieces, sb, sq)


from jax.sharding import Mesh
from jax.sharding import PartitionSpec as P

FEAT_AXES = ("feat_0", "feat_1")
DP = ("dp_0", "dp_1")
DP_FEAT = ("dp_0", "dp_1", "feat_0", "feat_1")


def exchange(x):
    return lax.all_to_all(x, FEAT_AXES, 0, 0, tiled=True)


def shift(x, by):
    size = lax.axis_size("dp_0")
    return lax.ppermute(x, "dp_0", [(i, (i + by) % size) for i in range(size)])


def swap(x):
    return lax.ppermute(x, "dp_1", [(0, 1), (1, 0)])


def around(x):
    half = x.shape[0] // 2
    left, right, mate = shift(x, 1), shift(x, -1), swap(x)
    far_a, far_b = shift(left[:half], 1), shift(right[half:], -1)
    left_mate, right_mate = swap(left), swap(right)
    return [x, mate, right, right_mate, far_a, far_b, swap(far_a), swap(far_b), left, left_mate]


def paired(parts, core):
    x, mate, right, right_mate, far_a, far_b, mate_a, mate_b, left, left_mate = parts
    swapped = core != 0
    pairs = []
    for one, two in (([x], [mate]), ([right], [right_mate]), ([far_a, far_b], [mate_a, mate_b]), ([left], [left_mate])):
        first = [jnp.where(swapped, v, u) for u, v in zip(one, two)]
        second = [jnp.where(swapped, u, v) for u, v in zip(one, two)]
        pairs.append(jnp.concatenate(first + second, axis=0))
    return pairs


def on_device(query_grads, build_grads, scored_grads):
    chip, core = lax.axis_index("dp_0"), lax.axis_index("dp_1")
    chips = lax.axis_size("dp_0")
    place = jnp.stack([chip, core]).astype(jnp.int32)
    size = lax.axis_size(FEAT_AXES)
    build_parts = around(build_grads)
    q_local = lax.all_to_all(query_grads, FEAT_AXES, split_axis=1, concat_axis=0, tiled=True)
    query_wide = q_local.astype(F32)
    squares = jnp.sum(query_wide * query_wide, axis=1)
    rows = jnp.concatenate([build_grads, q_local], axis=0)
    build_pairs = paired(build_parts, core)
    sums = jnp.zeros((chips, rows.shape[0], 2 * BLK), F32)
    for i, pair in enumerate(build_pairs):
        sums = lax.dynamic_update_slice(sums, across(rows, pair)[None], ((chip + i) % chips, 0, 0))
    after = (chip * 2 + core + 1) % (2 * chips)
    sums = lax.dynamic_update_slice(sums, squares[None, None], (after // 2, 0, after % 2 * BLK))
    q_local, sums = lax.optimization_barrier((q_local, sums))
    sums = jnp.sum(exchange(sums.reshape(size, -1, 2 * BLK)), axis=0)
    sums = exchange(jnp.broadcast_to(sums[None], (size, *sums.shape)))
    sum_parts = around(sums.reshape(-1, 2 * BLK))
    score_query = across(scored_grads, jnp.concatenate(paired(around(q_local), core), axis=0))
    score_build = across(scored_grads, jnp.concatenate(build_pairs, axis=0))
    partial_value = solve(place, sum_parts, score_build, score_query)
    partial_value = exchange(partial_value.reshape(size, -1, partial_value.shape[1]))
    return jnp.sum(partial_value.astype(F32), axis=0)


def solution(mesh):
    torus = Mesh(mesh.devices.reshape(4, 8, 4, 2), ("feat_0", "feat_1", "dp_0", "dp_1"))
    in_specs = (P(DP_FEAT, None), P(DP, FEAT_AXES), P(DP, FEAT_AXES))
    out_specs = P(DP_FEAT, None)
    return jax.shard_map(
        on_device, mesh=torus, in_specs=in_specs, out_specs=out_specs, check_vma=False
    )
```

```python
import functools
import jax, jax.numpy as jnp
from jax import lax
from jax.experimental import pallas as pl
from jax.experimental.pallas import tpu as pltpu

BLK = 128
FEAT = 131072
BF = jnp.bfloat16
F32 = jnp.float32

def split3(x):
    h = x.astype(BF)
    r = x - h.astype(F32)
    m = r.astype(BF)
    l = (r - m.astype(F32)).astype(BF)
    return h, m, l

def split2(x):
    h = x.astype(BF)
    return h, (x - h.astype(F32)).astype(BF)

def left6(x):
    h, m, l = split3(x)
    return jnp.concatenate([h, h, m, m, h, l], axis=1)

def right6(x):
    h, m, l = split3(x)
    return jnp.concatenate([h, m, h, m, l, h], axis=0)

def left4(x):
    h, m = split2(x)
    return jnp.concatenate([h, h, m, m], axis=1)

def mixed4(x):
    h, m = split2(x)
    return jnp.concatenate([h, m, h, m], axis=1)

def mm(a, b):
    return jnp.dot(a, b, preferred_element_type=F32)

def across(a, b):
    return lax.dot_general(a, b, (((1,), (1,)), ((), ())), preferred_element_type=F32)

def put_rows(x, j, row0, row1):
    g = j // 8 * 8
    sub = lax.broadcasted_iota(jnp.int32, (8, x.shape[1]), 0)
    block = jnp.where(sub == j - g, row0, jnp.where(sub == j - g + 1, row1, x[g:g+8]))
    parts = ([x[:g]] if g else []) + [block] + ([x[g+8:]] if g + 8 < x.shape[0] else [])
    return jnp.concatenate(parts, axis=0)

def sweep(p, off, tick):
    rows = p.shape[0]
    lane = lax.broadcasted_iota(jnp.int32, (1, p.shape[1]), 1)
    def spread(x, i):
        return jnp.broadcast_to(x[:, i:i+1], x.shape)
    c0, c1 = spread(p, off), spread(p, off + 1)
    for j in range(0, rows, 2):
        e, f, h = c0[j:j+1], c0[j+1:j+2], c1[j+1:j+2]
        inv = 1.0 / (e * h - f * f)
        i00, i01, i11 = h * inv, -f * inv, e * inv
        more = j + 2 < rows
        if more:
            d0, d1 = spread(p, off + j + 2), spread(p, off + j + 3)
            x0, x1 = c0[j+2:j+3], c1[j+2:j+3]
            y0, y1 = c0[j+3:j+4], c1[j+3:j+4]
            u0, u1 = i00 * x0 + i01 * x1, i01 * x0 + i11 * x1
            v0, v1 = i00 * y0 + i01 * y1, i01 * y0 + i11 * y1
            n0 = put_rows(d0 - c0 * u0 - c1 * u1, j, u0, u1)
            n1 = put_rows(d1 - c0 * v0 - c1 * v1, j, v0, v1)
        first, second = lane == off + j, lane == off + j + 1
        r0 = jnp.where(first, 1.0, jnp.where(second, 0.0, p[j:j+1]))
        r1 = jnp.where(first, 0.0, jnp.where(second, 1.0, p[j+1:j+2]))
        t0 = i00 * r0 + i01 * r1
        t1 = i01 * r0 + i11 * r1
        p = put_rows(jnp.where(first | second, 0.0, p) - c0 * t0 - c1 * t1, j, t0, t1)
        if more:
            c0, c1 = n0, n1
        tick()
    return p

def inverse(a, tick):
    n = a.shape[0]
    h = n // 2
    left = lax.broadcasted_iota(jnp.int32, (1, n), 1) < h
    top = sweep(a[:h], 0, tick)
    low = jnp.where(left, 0.0, a[h:]) - mm(left6(a[h:, :h]), right6(top))
    low = sweep(low, h, tick)
    high = jnp.where(left, top, 0.0) - mm(left6(top[:, h:]), right6(low))
    return jnp.concatenate([high, low], axis=0)

TILE = 256

class Spread:
    def __init__(self, tasks, steps):
        self.tasks, self.steps, self.step, self.done = tasks, steps, 0, 0
    def __call__(self):
        self.step += 1
        upto = len(self.tasks) * self.step // self.steps
        while self.done < upto:
            self.tasks[self.done]()
            self.done += 1

def solve_kernel(n, nq, place_ref, *refs):
    pieces, (sb_ref, sq_ref, out_ref, a, t, z, s, dinv, w, la, lt, lz, dq) = refs[:7], refs[7:]
    g = n // BLK
    ns = sb_ref.shape[0]
    qs = nq // g
    rows = BLK + qs
    tiles = n // TILE
    chip, core = place_ref[0], place_ref[1]
    chips = n // 256
    own, mate, right, left, side_mates, far, far_mate = pieces
    whole = chips * rows
    places = [(own, 0), (mate, 0), (right, 0), (side_mates, 0), (far, 0), (far_mate, 0), (left, 0), (side_mates, whole)]
    for dx in range(chips):
        there = lax.rem(chip + dx, chips)
        sc = pl.ds(pl.multiple_of(there * 2 * qs, 2 * qs), 2 * qs)
        zc = pl.ds(pl.multiple_of(there * 256, 256), 256)
        def score_rows(i, _, dx=dx, sc=sc, zc=zc):
            r = pl.ds(pl.multiple_of(i * 64, 64), 64)
            s[r, sc] = sq_ref[r, dx*2*qs:(dx+1)*2*qs]
            z[r, zc] = sb_ref[r, dx*256:(dx+1)*256]
            return 0
        lax.fori_loop(0, ns // 64, score_rows, 0)
        for flip in range(2):
            k = there * 2 + lax.rem(core + flip, 2)
            ks = pl.ds(pl.multiple_of(k * BLK, BLK), BLK)
            ts = pl.ds(pl.multiple_of(k * qs, qs), qs)
            ref, r0 = places[dx * 2 + flip]
            def columns(c, _, ref=ref, r0=r0, ks=ks, ts=ts):
                cs = pl.ds(pl.multiple_of(c * 256, 256), 256)
                a[ks, cs] = ref[pl.ds(pl.multiple_of(r0 + c * rows, 8), BLK), :]
                t[ts, cs] = ref[pl.ds(pl.multiple_of(r0 + c * rows + BLK, 8), qs), :]
                return 0
            lax.fori_loop(0, chips, columns, 0)
    tot = jnp.zeros((BLK, BLK), F32)
    eye = (lax.broadcasted_iota(jnp.int32, (BLK, BLK), 0) == lax.broadcasted_iota(jnp.int32, (BLK, BLK), 1)).astype(F32)
    blocks = [slice(k*BLK, (k+1)*BLK) for k in range(g)]
    squares = []
    for k in range(g):
        after = blocks[(k + 1) % g]
        squares.append(a[k*BLK:k*BLK+1, after][:, :qs])
        a[blocks[k], after] = jnp.transpose(a[after, blocks[k]])
        tot = tot + a[blocks[k], blocks[k]] * eye
    per = 256 // qs
    squares = [jnp.concatenate(squares[h*per:(h+1)*per], axis=1) for h in range(nq // 256)]
    trace = jnp.sum(jnp.sum(tot, axis=1, keepdims=True), axis=0, keepdims=True)
    damping = 0.1 * trace / (n * FEAT) + 1e-06
    for d in blocks:
        a[d, d] = a[d, d] + eye * (n * damping)
    dq[...] = jnp.zeros(dq.shape, F32)

    def strip(i):
        return slice(i * TILE, (i + 1) * TILE)

    def score_tasks(ks, d):
        d4 = right6(d)[:4*BLK]
        def dots(rt):
            r = strip(rt)
            lt[r, :] = left4(t[r, ks])
            dq[r, :] = dq[r, :] + mm(lt[r, :], d4) * t[r, ks]
        def scores(rt):
            r = strip(rt)
            lz[r, :] = left4(z[r, ks])
            v = mixed4(mm(lz[r, :], d4))
            for ct in range(nq // TILE):
                c = strip(ct)
                s[r, c] = s[r, c] - across(v, lt[c, :])
        return [functools.partial(dots, i) for i in range(nq // TILE)] + [functools.partial(scores, i) for i in range(ns // TILE)]

    def forward(lo, k, _):
        ks = pl.ds(pl.multiple_of(lax.rem(k + g - 1, g) * BLK, BLK), BLK)
        ns_ = pl.ds(pl.multiple_of(k * BLK, BLK), BLK)
        d = dinv[...]
        dl = left6(d)
        near = mm(dl, right6(a[ks, ns_]))
        block = a[ns_, ns_] - mm(left6(a[ns_, ks]), right6(near))

        def make_w(ct):
            c = strip(ct)
            cc = lax.broadcasted_iota(jnp.int32, (1, TILE), 1) + ct * TILE
            w[:, c] = right6(jnp.where(cc >= k * BLK, mm(dl, right6(a[ks, c])), 0.0))
        def make_la(rt):
            la[strip(rt), :] = left6(a[strip(rt), ks])
        def update(ref, left, terms, rt, ct):
            r, c = strip(rt), strip(ct)
            ref[r, c] = ref[r, c] - mm(left[r, :], w[:terms*BLK, c])
        tasks = [functools.partial(make_w, i) for i in range(lo, tiles)]
        tasks += [functools.partial(make_la, i) for i in range(lo, tiles)]
        tasks += score_tasks(ks, d)
        for ct in range(lo, tiles):
            tasks += [functools.partial(update, a, la, 6, rt, ct) for rt in range(lo, tiles)]
            tasks += [functools.partial(update, t, lt, 4, rt, ct) for rt in range(nq // TILE)]
            tasks += [functools.partial(update, z, lz, 4, rt, ct) for rt in range(ns // TILE)]
        tick = Spread(tasks, BLK // 2)
        dinv[...] = inverse(block, tick)
        return 0

    dinv[...] = jnp.zeros(dinv.shape, F32)
    for first, last, lo in SECTIONS:
        lax.fori_loop(first, last, functools.partial(forward, lo), 0)
    for task in score_tasks(slice(n - BLK, n), dinv[...]):
        task()

    ones = jnp.ones((8, 3 * BLK), BF)
    for h in range(nq // 256):
        c = strip(h)
        dots = across(ones, jnp.concatenate(split3(dq[c, :]), axis=1))[:1]
        self_score = (squares[h] - dots) / damping
        out_ref[:, c] = (s[:, c] * (1.0 / (damping * jnp.sqrt(self_score)))).astype(BF)

SECTIONS = ((0, 5, 0), (5, 8, 2))

def products_kernel(scored_ref, *refs):
    rows_refs, out_ref = refs[:-1], refs[-1]
    @pl.when(pl.program_id(0) == 0)
    def _():
        out_ref[...] = jnp.zeros(out_ref.shape, F32)
    def body(i, _):
        r = pl.ds(pl.multiple_of(i * 256, 256), 256)
        x = scored_ref[r, :]
        for j in range(out_ref.shape[1] // 256):
            each = len(rows_refs) * 256 // out_ref.shape[1]
            c = slice(j * 256, (j + 1) * 256)
            block = jnp.concatenate([ref[...] for ref in rows_refs[j*each:(j+1)*each]], axis=0)
            out_ref[r, c] = out_ref[r, c] + across(x, block)
        return 0
    lax.fori_loop(0, scored_ref.shape[0] // 256, body, 0)

def products(scored, groups):
    ns, width = scored.shape
    n = sum(x.shape[0] for x in groups)
    step = 1024
    cut = lambda x: pl.BlockSpec((x.shape[0], step), lambda i: (0, i))
    return pl.pallas_call(
        products_kernel,
        grid=(width // step,),
        out_shape=jax.ShapeDtypeStruct((ns, n), F32),
        in_specs=[cut(x) for x in (scored, *groups)],
        out_specs=pl.BlockSpec((ns, n), lambda i: (0, 0)),
        compiler_params=pltpu.CompilerParams(vmem_limit_bytes=32 * 1024 * 1024),
        cost_estimate=pl.CostEstimate(flops=2 * ns * width * n, bytes_accessed=2 * width * (ns + n), transcendentals=0),
        name="products",
    )(scored, *groups)

def solve(place, pieces, sb, sq):
    ns, n = sb.shape
    nq = sq.shape[1]
    vm = pl.BlockSpec(memory_space=pltpu.VMEM)
    return pl.pallas_call(
        functools.partial(solve_kernel, n, nq),
        out_shape=jax.ShapeDtypeStruct((ns, nq), BF),
        in_specs=[pl.BlockSpec(memory_space=pltpu.SMEM)] + [vm] * 9, out_specs=vm,
        scratch_shapes=[pltpu.VMEM((n, n), F32), pltpu.VMEM((nq, n), F32), pltpu.VMEM((ns, n), F32), pltpu.VMEM((ns, nq), F32),
                        pltpu.VMEM((BLK, BLK), F32), pltpu.VMEM((6*BLK, n), BF), pltpu.VMEM((n, 6*BLK), BF),
                        pltpu.VMEM((nq, 4*BLK), BF), pltpu.VMEM((ns, 4*BLK), BF), pltpu.VMEM((nq, BLK), F32)],
        compiler_params=pltpu.CompilerParams(vmem_limit_bytes=48 * 1024 * 1024),
        cost_estimate=pl.CostEstimate(flops=20_000_000_000, bytes_accessed=12_000_000, transcendentals=0),
        name="solve",
    )(place, *pieces, sb, sq)


from jax.sharding import Mesh
from jax.sharding import PartitionSpec as P

FEAT_AXES = ("feat_0", "feat_1")
DP = ("dp_0", "dp_1")
DP_FEAT = ("dp_0", "dp_1", "feat_0", "feat_1")


def exchange(x):
    return lax.all_to_all(x, FEAT_AXES, 0, 0, tiled=True)


def shift(x, by):
    size = lax.axis_size("dp_0")
    return lax.ppermute(x, "dp_0", [(i, (i + by) % size) for i in range(size)])


def swap(x):
    return lax.ppermute(x, "dp_1", [(0, 1), (1, 0)])


def beside(x):
    return shift(x, 1), shift(x, -1)


def beyond(left, right):
    half = left.shape[0] // 2
    return jnp.concatenate([shift(left[:half], 1), shift(right[half:], -1)], axis=0)


def paired(parts, core):
    x, mate, right, left, side_mates, far, far_mate = parts
    swapped, count = core != 0, x.shape[0]
    pairs = []
    for one, two in ((x, mate), (right, side_mates[:count]), (far, far_mate), (left, side_mates[count:])):
        pairs += [jnp.where(swapped, two, one), jnp.where(swapped, one, two)]
    return pairs


def on_device(query_grads, build_grads, scored_grads):
    chip, core = lax.axis_index("dp_0"), lax.axis_index("dp_1")
    chips = lax.axis_size("dp_0")
    place = jnp.stack([chip, core]).astype(jnp.int32)
    size = lax.axis_size(FEAT_AXES)
    mate = swap(build_grads)
    left, right = beside(build_grads)
    q_local = lax.all_to_all(query_grads, FEAT_AXES, split_axis=1, concat_axis=0, tiled=True)
    left, right, q_local = lax.optimization_barrier((left, right, q_local))
    far = beyond(left, right)
    sides = swap(jnp.concatenate([right, left], axis=0))
    build_parts = [build_grads, mate, right, left, sides, far, swap(far)]
    query_wide = q_local.astype(F32)
    squares = jnp.sum(query_wide * query_wide, axis=1)
    rows = jnp.concatenate([build_grads, q_local], axis=0)
    build_pairs = paired(build_parts, core)
    sums = jnp.zeros((chips, rows.shape[0], 2 * BLK), F32)
    for i in range(chips):
        pair = jnp.concatenate(build_pairs[2 * i:2 * i + 2], axis=0)
        sums = lax.dynamic_update_slice(sums, across(rows, pair)[None], ((chip + i) % chips, 0, 0))
    after = (chip * 2 + core + 1) % (2 * chips)
    sums = lax.dynamic_update_slice(sums, squares[None, None], (after // 2, 0, after % 2 * BLK))
    q_local, sums = lax.optimization_barrier((q_local, sums))
    q_left, q_right = beside(q_local)
    sums = jnp.sum(exchange(sums.reshape(size, -1, 2 * BLK)), axis=0)
    sums, q_left, q_right = lax.optimization_barrier((sums, q_left, q_right))
    q_far = shift(q_left, 1)
    sums = exchange(jnp.broadcast_to(sums[None], (size, *sums.shape))).reshape(-1, 2 * BLK)
    straight = jnp.concatenate([q_local, q_right, q_far, q_left], axis=0)
    sums, straight, scored_grads = lax.optimization_barrier((sums, straight, scored_grads))
    left, right = beside(sums)
    mate = swap(sums)
    crossed = swap(straight)
    score_build = products(scored_grads, build_pairs)
    left, right, crossed, score_build = lax.optimization_barrier((left, right, crossed, score_build))
    far = beyond(left, right)
    sides = swap(jnp.concatenate([right, left], axis=0))
    blocks = lambda x: x.reshape(chips, -1, x.shape[1])
    first = jnp.where(core == 0, straight, crossed)
    second = jnp.where(core == 0, crossed, straight)
    query_all = jnp.concatenate([blocks(first), blocks(second)], axis=1).reshape(2, -1, first.shape[1])
    score_query = products(scored_grads, [query_all[0], query_all[1]])
    far, score_query = lax.optimization_barrier((far, score_query))
    partial_value = solve(place, [sums, mate, right, left, sides, far, swap(far)], score_build, score_query)
    partial_value = exchange(partial_value.reshape(size, -1, partial_value.shape[1]))
    return jnp.sum(partial_value.astype(F32), axis=0)


def solution(mesh):
    torus = Mesh(mesh.devices.reshape(4, 8, 4, 2), ("feat_0", "feat_1", "dp_0", "dp_1"))
    in_specs = (P(DP_FEAT, None), P(DP, FEAT_AXES), P(DP, FEAT_AXES))
    out_specs = P(DP_FEAT, None)
    return jax.shard_map(
        on_device, mesh=torus, in_specs=in_specs, out_specs=out_specs, check_vma=False
    )
```

```python
import functools
import jax, jax.numpy as jnp
from jax import lax
from jax.experimental import pallas as pl
from jax.experimental.pallas import tpu as pltpu

BLK = 128
FEAT = 131072
BF = jnp.bfloat16
F32 = jnp.float32

def split3(x):
    h = x.astype(BF)
    r = x - h.astype(F32)
    m = r.astype(BF)
    l = (r - m.astype(F32)).astype(BF)
    return h, m, l

def split2(x):
    h = x.astype(BF)
    return h, (x - h.astype(F32)).astype(BF)

def left6(x):
    h, m, l = split3(x)
    return jnp.concatenate([h, h, m, m, h, l], axis=1)

def right6(x):
    h, m, l = split3(x)
    return jnp.concatenate([h, m, h, m, l, h], axis=0)

def left4(x):
    h, m = split2(x)
    return jnp.concatenate([h, h, m, m], axis=1)

def mixed4(x):
    h, m = split2(x)
    return jnp.concatenate([h, m, h, m], axis=1)

def mm(a, b):
    return jnp.dot(a, b, preferred_element_type=F32)

def across(a, b):
    return lax.dot_general(a, b, (((1,), (1,)), ((), ())), preferred_element_type=F32)

def put_rows(x, j, row0, row1):
    g = j // 8 * 8
    sub = lax.broadcasted_iota(jnp.int32, (8, x.shape[1]), 0)
    block = jnp.where(sub == j - g, row0, jnp.where(sub == j - g + 1, row1, x[g:g+8]))
    parts = ([x[:g]] if g else []) + [block] + ([x[g+8:]] if g + 8 < x.shape[0] else [])
    return jnp.concatenate(parts, axis=0)

def sweep(p, off, tick):
    rows = p.shape[0]
    lane = lax.broadcasted_iota(jnp.int32, (1, p.shape[1]), 1)
    def spread(x, i):
        return jnp.broadcast_to(x[:, i:i+1], x.shape)
    c0, c1 = spread(p, off), spread(p, off + 1)
    for j in range(0, rows, 2):
        e, f, h = c0[j:j+1], c0[j+1:j+2], c1[j+1:j+2]
        inv = 1.0 / (e * h - f * f)
        i00, i01, i11 = h * inv, -f * inv, e * inv
        more = j + 2 < rows
        if more:
            d0, d1 = spread(p, off + j + 2), spread(p, off + j + 3)
            x0, x1 = c0[j+2:j+3], c1[j+2:j+3]
            y0, y1 = c0[j+3:j+4], c1[j+3:j+4]
            u0, u1 = i00 * x0 + i01 * x1, i01 * x0 + i11 * x1
            v0, v1 = i00 * y0 + i01 * y1, i01 * y0 + i11 * y1
            n0 = put_rows(d0 - c0 * u0 - c1 * u1, j, u0, u1)
            n1 = put_rows(d1 - c0 * v0 - c1 * v1, j, v0, v1)
        first, second = lane == off + j, lane == off + j + 1
        r0 = jnp.where(first, 1.0, jnp.where(second, 0.0, p[j:j+1]))
        r1 = jnp.where(first, 0.0, jnp.where(second, 1.0, p[j+1:j+2]))
        t0 = i00 * r0 + i01 * r1
        t1 = i01 * r0 + i11 * r1
        p = put_rows(jnp.where(first | second, 0.0, p) - c0 * t0 - c1 * t1, j, t0, t1)
        if more:
            c0, c1 = n0, n1
        tick()
    return p

def inverse(a, tick):
    n = a.shape[0]
    h = n // 2
    left = lax.broadcasted_iota(jnp.int32, (1, n), 1) < h
    top = sweep(a[:h], 0, tick)
    low = jnp.where(left, 0.0, a[h:]) - mm(left6(a[h:, :h]), right6(top))
    low = sweep(low, h, tick)
    high = jnp.where(left, top, 0.0) - mm(left6(top[:, h:]), right6(low))
    return jnp.concatenate([high, low], axis=0)

TILE = 256

class Spread:
    def __init__(self, tasks, steps):
        self.tasks, self.steps, self.step, self.done = tasks, steps, 0, 0
    def __call__(self):
        self.step += 1
        upto = len(self.tasks) * self.step // self.steps
        while self.done < upto:
            self.tasks[self.done]()
            self.done += 1

def solve_kernel(n, nq, place_ref, *refs):
    pieces, (sb_ref, sq_ref, out_ref, a, t, z, s, dinv, w, la, lt, lz, dq) = refs[:7], refs[7:]
    g = n // BLK
    ns = sb_ref.shape[0]
    qs = nq // g
    rows = BLK + qs
    tiles = n // TILE
    chip, core = place_ref[0], place_ref[1]
    chips = n // 256
    own, mate, right, left, side_mates, far, far_mate = pieces
    whole = chips * rows
    places = [(own, 0), (mate, 0), (right, 0), (side_mates, 0), (far, 0), (far_mate, 0), (left, 0), (side_mates, whole)]
    for dx in range(chips):
        there = lax.rem(chip + dx, chips)
        sc = pl.ds(pl.multiple_of(there * 2 * qs, 2 * qs), 2 * qs)
        zc = pl.ds(pl.multiple_of(there * 256, 256), 256)
        def score_rows(i, _, dx=dx, sc=sc, zc=zc):
            r = pl.ds(pl.multiple_of(i * 64, 64), 64)
            s[r, sc] = sq_ref[r, dx*2*qs:(dx+1)*2*qs]
            z[r, zc] = sb_ref[r, dx*256:(dx+1)*256]
            return 0
        lax.fori_loop(0, ns // 64, score_rows, 0)
        for flip in range(2):
            k = there * 2 + lax.rem(core + flip, 2)
            ks = pl.ds(pl.multiple_of(k * BLK, BLK), BLK)
            ts = pl.ds(pl.multiple_of(k * qs, qs), qs)
            ref, r0 = places[dx * 2 + flip]
            def columns(c, _, ref=ref, r0=r0, ks=ks, ts=ts):
                cs = pl.ds(pl.multiple_of(c * 256, 256), 256)
                a[ks, cs] = ref[pl.ds(pl.multiple_of(r0 + c * rows, 8), BLK), :]
                t[ts, cs] = ref[pl.ds(pl.multiple_of(r0 + c * rows + BLK, 8), qs), :]
                return 0
            lax.fori_loop(0, chips, columns, 0)
    tot = jnp.zeros((BLK, BLK), F32)
    eye = (lax.broadcasted_iota(jnp.int32, (BLK, BLK), 0) == lax.broadcasted_iota(jnp.int32, (BLK, BLK), 1)).astype(F32)
    blocks = [slice(k*BLK, (k+1)*BLK) for k in range(g)]
    squares = []
    for k in range(g):
        after = blocks[(k + 1) % g]
        squares.append(a[k*BLK:k*BLK+1, after][:, :qs])
        a[blocks[k], after] = jnp.transpose(a[after, blocks[k]])
        tot = tot + a[blocks[k], blocks[k]] * eye
    per = 256 // qs
    squares = [jnp.concatenate(squares[h*per:(h+1)*per], axis=1) for h in range(nq // 256)]
    trace = jnp.sum(jnp.sum(tot, axis=1, keepdims=True), axis=0, keepdims=True)
    damping = 0.1 * trace / (n * FEAT) + 1e-06
    for d in blocks:
        a[d, d] = a[d, d] + eye * (n * damping)
    dq[...] = jnp.zeros(dq.shape, F32)

    def strip(i):
        return slice(i * TILE, (i + 1) * TILE)

    def score_tasks(ks, d):
        d4 = right6(d)[:4*BLK]
        def dots(rt):
            r = strip(rt)
            lt[r, :] = left4(t[r, ks])
            dq[r, :] = dq[r, :] + mm(lt[r, :], d4) * t[r, ks]
        def scores(rt):
            r = strip(rt)
            lz[r, :] = left4(z[r, ks])
            v = mixed4(mm(lz[r, :], d4))
            for ct in range(nq // TILE):
                c = strip(ct)
                s[r, c] = s[r, c] - across(v, lt[c, :])
        return [functools.partial(dots, i) for i in range(nq // TILE)] + [functools.partial(scores, i) for i in range(ns // TILE)]

    def forward(lo, k, _):
        ks = pl.ds(pl.multiple_of(lax.rem(k + g - 1, g) * BLK, BLK), BLK)
        ns_ = pl.ds(pl.multiple_of(k * BLK, BLK), BLK)
        d = dinv[...]
        dl = left6(d)
        near = mm(dl, right6(a[ks, ns_]))
        block = a[ns_, ns_] - mm(left6(a[ns_, ks]), right6(near))

        def make_w(ct):
            c = strip(ct)
            cc = lax.broadcasted_iota(jnp.int32, (1, TILE), 1) + ct * TILE
            w[:, c] = right6(jnp.where(cc >= k * BLK, mm(dl, right6(a[ks, c])), 0.0))
        def make_la(rt):
            la[strip(rt), :] = left6(a[strip(rt), ks])
        def update(ref, left, terms, rt, ct):
            r, c = strip(rt), strip(ct)
            ref[r, c] = ref[r, c] - mm(left[r, :], w[:terms*BLK, c])
        tasks = [functools.partial(make_w, i) for i in range(lo, tiles)]
        tasks += [functools.partial(make_la, i) for i in range(lo, tiles)]
        tasks += score_tasks(ks, d)
        for ct in range(lo, tiles):
            tasks += [functools.partial(update, a, la, 6, rt, ct) for rt in range(lo, tiles)]
            tasks += [functools.partial(update, t, lt, 4, rt, ct) for rt in range(nq // TILE)]
            tasks += [functools.partial(update, z, lz, 4, rt, ct) for rt in range(ns // TILE)]
        tick = Spread(tasks, BLK // 2)
        dinv[...] = inverse(block, tick)
        return 0

    dinv[...] = jnp.zeros(dinv.shape, F32)
    for first, last, lo in SECTIONS:
        lax.fori_loop(first, last, functools.partial(forward, lo), 0)
    for task in score_tasks(slice(n - BLK, n), dinv[...]):
        task()

    ones = jnp.ones((8, 3 * BLK), BF)
    for h in range(nq // 256):
        c = strip(h)
        dots = across(ones, jnp.concatenate(split3(dq[c, :]), axis=1))[:1]
        self_score = (squares[h] - dots) / damping
        out_ref[:, c] = (s[:, c] * (1.0 / (damping * jnp.sqrt(self_score)))).astype(BF)

SECTIONS = ((0, 5, 0), (5, 8, 2))

def products_kernel(scored_ref, *refs):
    rows_refs, out_ref = refs[:-1], refs[-1]
    @pl.when(pl.program_id(0) == 0)
    def _():
        out_ref[...] = jnp.zeros(out_ref.shape, F32)
    def body(i, _):
        r = pl.ds(pl.multiple_of(i * 256, 256), 256)
        x = scored_ref[r, :]
        for j in range(out_ref.shape[1] // 256):
            each = len(rows_refs) * 256 // out_ref.shape[1]
            c = slice(j * 256, (j + 1) * 256)
            block = jnp.concatenate([ref[...] for ref in rows_refs[j*each:(j+1)*each]], axis=0)
            out_ref[r, c] = out_ref[r, c] + across(x, block)
        return 0
    lax.fori_loop(0, scored_ref.shape[0] // 256, body, 0)

def products(scored, groups):
    ns, width = scored.shape
    n = sum(x.shape[0] for x in groups)
    step = 1024
    cut = lambda x: pl.BlockSpec((x.shape[0], step), lambda i: (0, i))
    return pl.pallas_call(
        products_kernel,
        grid=(width // step,),
        out_shape=jax.ShapeDtypeStruct((ns, n), F32),
        in_specs=[cut(x) for x in (scored, *groups)],
        out_specs=pl.BlockSpec((ns, n), lambda i: (0, 0)),
        compiler_params=pltpu.CompilerParams(vmem_limit_bytes=54 * 1024 * 1024),
        cost_estimate=pl.CostEstimate(flops=2 * ns * width * n, bytes_accessed=2 * width * (ns + n), transcendentals=0),
        name="products",
    )(scored, *groups)

def solve(place, pieces, sb, sq):
    ns, n = sb.shape
    nq = sq.shape[1]
    vm = pl.BlockSpec(memory_space=pltpu.VMEM)
    return pl.pallas_call(
        functools.partial(solve_kernel, n, nq),
        out_shape=jax.ShapeDtypeStruct((ns, nq), BF),
        in_specs=[pl.BlockSpec(memory_space=pltpu.SMEM)] + [vm] * 9, out_specs=vm,
        scratch_shapes=[pltpu.VMEM((n, n), F32), pltpu.VMEM((nq, n), F32), pltpu.VMEM((ns, n), F32), pltpu.VMEM((ns, nq), F32),
                        pltpu.VMEM((BLK, BLK), F32), pltpu.VMEM((6*BLK, n), BF), pltpu.VMEM((n, 6*BLK), BF),
                        pltpu.VMEM((nq, 4*BLK), BF), pltpu.VMEM((ns, 4*BLK), BF), pltpu.VMEM((nq, BLK), F32)],
        compiler_params=pltpu.CompilerParams(vmem_limit_bytes=48 * 1024 * 1024),
        cost_estimate=pl.CostEstimate(flops=20_000_000_000, bytes_accessed=12_000_000, transcendentals=0),
        name="solve",
    )(place, *pieces, sb, sq)


from jax.sharding import Mesh
from jax.sharding import PartitionSpec as P

FEAT_AXES = ("feat_0", "feat_1")
DP = ("dp_0", "dp_1")
DP_FEAT = ("dp_0", "dp_1", "feat_0", "feat_1")


def exchange(x):
    return lax.all_to_all(x, FEAT_AXES, 0, 0, tiled=True)


def shift(x, by):
    size = lax.axis_size("dp_0")
    return lax.ppermute(x, "dp_0", [(i, (i + by) % size) for i in range(size)])


def swap(x):
    return lax.ppermute(x, "dp_1", [(0, 1), (1, 0)])


def beside(x):
    return shift(x, 1), shift(x, -1)


def beyond(left, right):
    half = left.shape[0] // 2
    return jnp.concatenate([shift(left[:half], 1), shift(right[half:], -1)], axis=0)


def ordered(one, two, core):
    return [jnp.where(core != 0, two, one), jnp.where(core != 0, one, two)]


def on_device(query_grads, build_grads, scored_grads):
    chip, core = lax.axis_index("dp_0"), lax.axis_index("dp_1")
    chips = lax.axis_size("dp_0")
    place = jnp.stack([chip, core]).astype(jnp.int32)
    size = lax.axis_size(FEAT_AXES)
    mate = swap(build_grads)
    left, right = beside(build_grads)
    q_local = lax.all_to_all(query_grads, FEAT_AXES, split_axis=1, concat_axis=0, tiled=True)
    left, right, q_local = lax.optimization_barrier((left, right, q_local))
    sides = swap(jnp.concatenate([right, left], axis=0))
    far = beyond(left, right)
    query_wide = q_local.astype(F32)
    squares = jnp.sum(query_wide * query_wide, axis=1)
    rows = jnp.concatenate([build_grads, q_local], axis=0)
    count = build_grads.shape[0]
    near = [ordered(build_grads, mate, core), ordered(right, sides[:count], core), ordered(left, sides[count:], core)]
    sums = jnp.zeros((chips, rows.shape[0], 2 * BLK), F32)

    def placed(sums, pair, step):
        value = across(rows, jnp.concatenate(pair, axis=0))
        return lax.dynamic_update_slice(sums, value[None], ((chip + step) % chips, 0, 0))

    for step, pair in zip((0, 1, 3), near):
        sums = placed(sums, pair, step)
    far, sums = lax.optimization_barrier((far, sums))
    distant = ordered(far, swap(far), core)
    sums = placed(sums, distant, 2)
    build_pairs = near[0] + near[1] + distant + near[2]
    after = (chip * 2 + core + 1) % (2 * chips)
    sums = lax.dynamic_update_slice(sums, squares[None, None], (after // 2, 0, after % 2 * BLK))
    q_local, sums = lax.optimization_barrier((q_local, sums))
    q_left, q_right = beside(q_local)
    sums = jnp.sum(exchange(sums.reshape(size, -1, 2 * BLK)), axis=0)
    sums, q_left, q_right, scored_grads = lax.optimization_barrier((sums, q_left, q_right, scored_grads))
    q_far = shift(q_left, 1)
    sums = exchange(jnp.broadcast_to(sums[None], (size, *sums.shape))).reshape(-1, 2 * BLK)
    straight = jnp.concatenate([q_local, q_right, q_far, q_left], axis=0)
    score_build = products(scored_grads, build_pairs)
    sums, straight, score_build = lax.optimization_barrier((sums, straight, score_build))
    left, right = beside(sums)
    mate = swap(sums)
    crossed = swap(straight)
    left, right, crossed = lax.optimization_barrier((left, right, crossed))
    far = beyond(left, right)
    sides = swap(jnp.concatenate([right, left], axis=0))
    blocks = lambda x: x.reshape(chips, -1, x.shape[1])
    first = jnp.where(core == 0, straight, crossed)
    second = jnp.where(core == 0, crossed, straight)
    query_all = jnp.concatenate([blocks(first), blocks(second)], axis=1).reshape(2, -1, first.shape[1])
    score_query = products(scored_grads, [query_all[0], query_all[1]])
    far, score_query = lax.optimization_barrier((far, score_query))
    partial_value = solve(place, [sums, mate, right, left, sides, far, swap(far)], score_build, score_query)
    partial_value = exchange(partial_value.reshape(size, -1, partial_value.shape[1]))
    return jnp.sum(partial_value.astype(F32), axis=0)


def solution(mesh):
    torus = Mesh(mesh.devices.reshape(4, 8, 4, 2), ("feat_0", "feat_1", "dp_0", "dp_1"))
    in_specs = (P(DP_FEAT, None), P(DP, FEAT_AXES), P(DP, FEAT_AXES))
    out_specs = P(DP_FEAT, None)

    return jax.shard_map(on_device, mesh=torus, in_specs=in_specs, out_specs=out_specs, check_vma=False)
```
